32 devices in a mesh: seq: 16 (over z, y, core), cfg: 2 (over x).
Axes of the slice: x: 2, y: 2, z: 4, core: 2. Of those that a mesh axis runs over, the one named last changes fastest.
Arguments:
- queries: bfloat16 [8192, 2560], P(('cfg', 'seq')), parts along dimension 0, may hold values from -40 to 40
- latent_keys: bfloat16 [8192, 2560], P(('cfg', 'seq')), parts along dimension 0, may hold values from -6 to 6
- latent_values: bfloat16 [8192, 2560], P(('cfg', 'seq')), parts along dimension 0, may hold values from -6 to 6
- prompt_keyvals: bfloat16 [2, 2048, 2560], P(None, ('cfg', 'seq')), parts along dimension 1, may hold values from -9 to 9
- block_lists: int32 [32, 8], P('seq'), may hold values from -1 to 31, as said below
- tile_segment: int32 [16], P('seq'), may hold values from 0 to 3
Outputs:
- attended: bfloat16 [8192, 2560], P(('cfg', 'seq')), parts along dimension 0
The draws below stay inside these ranges and needn't reach their ends.
There are 2 independent parts, one for each index of `cfg`. The reference program is written for one: setup_inputs(seed, part) draws one part's arguments, and reference() takes and returns one part's arrays. A program takes and returns all parts, laid end to end along the dimension named above; an argument that names none is the same for every part. Nothing has to cross between parts.
Inputs may be any that keep to these rules, and one draw needn't show every extreme that they name: `block_lists`: row b lists distinct key blocks, all held by indices of seq at most 3 away from the one holding query block b (each index holds 2 blocks in order); b itself comes first, used entries precede the -1 entries, and some row fills all 8.
All inputs are finite; a program needn't handle non-finite values.
Results may differ from the reference program's by a relative error of at most 0.0035.
Values may be sent and summed in bfloat16 or wider, within the bound.
A program may use at most 128 MiB of HBM per device.

```python
import math
import jax
import jax.numpy as jnp
from jax import lax

HEADS = 20
HD = 128
TOK_DEV = 256
BLK = 128
REACH = 3
SLOTS = 8
SEGS = 4
TXT = 256
TOKENS = 4096
QBLOCKS = 32
TILES = 16
TXT_ALL = 1024


def shared_keys(key):
    base = jax.random.fold_in(key, 11)
    values = jnp.clip(jax.random.normal(base, (TOKENS, HEADS * HD), jnp.float32), -6.0, 6.0)
    return values


def draw_latent_keys(key, part):
    return shared_keys(key).astype(jnp.bfloat16)


def draw_queries(key, part):
    own = jnp.clip(jax.random.normal(jax.random.fold_in(key, 23), (TOKENS, HEADS * HD), jnp.float32), -6.0, 6.0)
    return own.astype(jnp.bfloat16)


def draw_tile_segment(key, part):
    key_base, key_pick = jax.random.split(jax.random.fold_in(key, 47), 2)
    segment_ids = jax.random.randint(key_base, (TILES,), 0, SEGS)
    chosen_tile = jax.random.randint(key_pick, (), 0, TILES)
    far_tile = (chosen_tile + TILES // 2) % TILES
    far_segment = far_tile * SEGS // TILES
    tiles_all = jnp.arange(TILES, dtype=jnp.int32)
    segment_ids = jnp.where(tiles_all == chosen_tile, far_segment, segment_ids)
    return segment_ids.astype(jnp.int32)


def draw_block_lists(key, part):
    per_device = TOK_DEV // BLK
    window = (2 * REACH + 1) * per_device
    rows = jnp.arange(QBLOCKS, dtype=jnp.int32)
    device = rows // per_device
    places = jnp.arange(window, dtype=jnp.int32)
    candidate = (device[:, None] - REACH) * per_device + places[None, :]
    valid = (candidate >= 0) & (candidate < QBLOCKS)
    distance = jnp.abs(places // per_device - REACH)
    key_noise, key_count, key_full, key_heavy = jax.random.split(jax.random.fold_in(key, 31), 4)
    noise = jax.random.randint(key_noise, (QBLOCKS, window), 0, 1000)
    score = noise - 250 * distance[None, :]
    score = jnp.where(candidate == rows[:, None], 100000, score)
    score = jnp.where(valid, score, -100000)
    score = score * window + places[None, :]
    unused, order = lax.top_k(score, SLOTS)
    chosen = jnp.take_along_axis(candidate, order, axis=1)
    chosen_valid = jnp.take_along_axis(valid, order, axis=1)
    heavy = jax.random.randint(key_heavy, (QBLOCKS // per_device,), 0, 4)
    light = jax.random.randint(key_count, (QBLOCKS,), SLOTS // 2, SLOTS)
    count = jnp.where(heavy[device] == 0, SLOTS, light)
    full_row = jax.random.randint(key_full, (), QBLOCKS // 2 - per_device, QBLOCKS // 2)
    count = jnp.where(rows == full_row, SLOTS, count)
    slot = jnp.arange(SLOTS, dtype=jnp.int32)
    keep = (slot[None, :] < count[:, None]) & chosen_valid
    return jnp.where(keep, chosen, -1).astype(jnp.int32)


def levels(own_key, dims, pieces, smallest, top_value):
    level, own = 1.0, jax.random.fold_in(own_key, 6)
    for dim, shards_of in pieces:
        steps = jnp.exp(jax.random.uniform(jax.random.fold_in(own, dim), (shards_of,), jnp.float32, smallest / len(pieces), top_value / len(pieces)))
        level = level * jnp.repeat(steps, dims[dim] // shards_of).reshape([-1 if axis == dim else 1 for axis in range(len(dims))])
    return level


def centred(rng, shape, deviation, reach, shards=(), held_as=jnp.bfloat16):
    array = deviation * jax.random.normal(rng, shape, jnp.float32)
    if shards:
        array = array * levels(rng, shape, shards, -0.22, 0.18)
    return jnp.clip(array, -reach, reach).astype(held_as)


def setup_inputs(seed: int = 0, part: int = 0) -> dict:
    key_of = jax.random.split(jax.random.key(seed), 7)
    part_keys = jax.random.split(jax.random.fold_in(key_of[6], part), 7)
    queries = draw_queries(jax.random.fold_in(jax.random.fold_in(key_of[6], part), 71), part)
    latent_keys = draw_latent_keys(jax.random.fold_in(jax.random.fold_in(key_of[6], part), 71), part)
    latent_values = centred(part_keys[2], (TOKENS, HEADS * HD), 1.0, 6.0, ((0, 16),))
    prompt_keyvals = centred(part_keys[3], (2, TXT_ALL, HEADS * HD), 1.5, 9.0, ((1, 16),))
    block_lists = draw_block_lists(jax.random.fold_in(key_of[6], 71), part)
    tile_segment = draw_tile_segment(jax.random.fold_in(key_of[6], 71), part)
    return {"queries": queries, "latent_keys": latent_keys, "latent_values": latent_values, "prompt_keyvals": prompt_keyvals, "block_lists": block_lists, "tile_segment": tile_segment}


def reference(queries, latent_keys, latent_values, prompt_keyvals, block_lists, tile_segment):
    per_device = TOK_DEV // BLK
    width = HEADS * HD
    scale = 1.0 / math.sqrt(HD)
    key_blocks = latent_keys.reshape(QBLOCKS, BLK, width)
    value_blocks = latent_values.reshape(QBLOCKS, BLK, width)
    query_blocks = queries.reshape(QBLOCKS, BLK, width)

    def one_block(index):
        lists = block_lists[index]
        valid = lists >= 0
        safe = jnp.where(valid, lists, 0).astype(jnp.int32)
        keys_sel = key_blocks[safe].reshape(SLOTS * BLK, width)
        values_sel = value_blocks[safe].reshape(SLOTS * BLK, width)
        segment = tile_segment[index // per_device]
        start = (segment * TXT).astype(jnp.int32)
        text_keys = lax.dynamic_slice_in_dim(prompt_keyvals[0], start, TXT, 0)
        text_values = lax.dynamic_slice_in_dim(prompt_keyvals[1], start, TXT, 0)
        all_keys = jnp.concatenate([keys_sel, text_keys], axis=0).astype(jnp.float32)
        all_values = jnp.concatenate([values_sel, text_values], axis=0).astype(jnp.float32)
        allowed = jnp.concatenate([jnp.repeat(valid, BLK), jnp.ones((TXT,), dtype=bool)])
        query_f = query_blocks[index].astype(jnp.float32).reshape(BLK, HEADS, HD)
        key_f = all_keys.reshape(-1, HEADS, HD)
        value_f = all_values.reshape(-1, HEADS, HD)
        scores = jnp.einsum('qhd,khd->hqk', query_f, key_f) * scale
        mask = allowed[None, None, :]
        top = lax.optimization_barrier(jnp.max(jnp.where(mask, scores, -jnp.inf), axis=2, keepdims=True))
        weights = jnp.where(mask, jnp.exp(scores - top), 0.0)
        total = lax.optimization_barrier(jnp.sum(weights, axis=2, keepdims=True))
        rounded = lax.optimization_barrier(weights.astype(jnp.bfloat16)).astype(jnp.float32)
        mixed = jnp.einsum('hqk,khd->hqd', rounded, value_f) / total
        return jnp.transpose(mixed, (1, 0, 2)).reshape(BLK, width).astype(jnp.bfloat16)
    result = lax.map(one_block, jnp.arange(QBLOCKS, dtype=jnp.int32))
    return result.reshape(TOKENS, width)
```

```python
import functools
import math

import jax
import jax.numpy as jnp
from jax import lax
from jax.experimental import pallas as pl
from jax.experimental.pallas import tpu as pltpu
from jax.sharding import PartitionSpec as P

HD = 128
BLK = 128
REACH = 3
TXT = 256
MESH = pl.DeviceIdType.MESH


def kernel(n, G, H, S, T, pregathered, info_ref, q_ref, k_ref, v_ref, t_ref, out_ref, *scratch):
    NG = n // G
    PB = q_ref.shape[0]
    kv = scratch[:H]
    qb = scratch[H : 2 * H]
    ob = scratch[2 * H : 3 * H]
    (txt, ibuf, ismem, p1s, p1r, loc, t1s, t1r, tls, is_, ir, il, ism,
     zs, zr, ths, thr, os_, or_, ol) = scratch[3 * H :]
    me = lax.axis_index("seq")
    grp = me // G
    r = me % G
    first = grp * G
    has_up = grp + 1 < NG
    has_dn = grp > 0
    up, dn = me + G, me - G

    def remote(src, dst, ss, rs, dev):
        return pltpu.make_async_remote_copy(
            src_ref=src, dst_ref=dst, send_sem=ss, recv_sem=rs,
            device_id={"seq": dev}, device_id_type=MESH)

    def head_cols(t, h):
        return pl.ds(pl.multiple_of((t * H + h) * HD, HD), HD)

    def group_cols(t):
        return pl.ds(pl.multiple_of(t * (H * HD), HD), H * HD)

    barrier = pltpu.get_barrier_semaphore()
    for p in range(1, G):
        pl.semaphore_signal(barrier, inc=1, device_id={"seq": first + (r + p) % G}, device_id_type=MESH)

    @pl.when(has_up)
    def _():
        pl.semaphore_signal(barrier, inc=1, device_id={"seq": up}, device_id_type=MESH)

    @pl.when(has_dn)
    def _():
        pl.semaphore_signal(barrier, inc=1, device_id={"seq": dn}, device_id_type=MESH)

    count = (G - 1) + has_up.astype(jnp.int32) + has_dn.astype(jnp.int32)
    pl.semaphore_wait(barrier, count)

    trows = t_ref.shape[1]
    grows = trows if pregathered else trows * G

    def text_at(row, rows):
        return txt.at[:, row // TXT, pl.ds(pl.multiple_of(row % TXT, min(rows, TXT)), rows), :]

    def text_group(g):
        return text_at(g * grows, grows)

    def text_own(src_r, dst_t, p):
        row = (first + src_r) * trows
        return remote(t_ref.at[:, :, group_cols(dst_t)], text_at(row, trows),
                      t1s.at[p - 1], t1r.at[p - 1], first + dst_t)

    def info_own(src_r, dst_t, p):
        return remote(info_ref, ibuf.at[src_r], is_.at[p - 1], ir.at[p - 1], first + dst_t)

    def slot_ref(h, a, tile):
        blocks = pl.ds(tile * PB, PB)
        if a == 2:
            return qb[h].at[blocks]
        return kv[h].at[a, pl.ds((REACH + tile) * PB, PB)]

    def p1(h, a, src_r, dst_t, p):
        src = (k_ref, v_ref, q_ref)[a].at[:, :, head_cols(dst_t, h)]
        return remote(src, slot_ref(h, a, src_r), p1s.at[h, a, p - 1], p1r.at[h, a, p - 1], first + dst_t)

    def p1_local(h, a):
        src = (k_ref, v_ref, q_ref)[a].at[:, :, head_cols(r, h)]
        return pltpu.make_async_copy(src, slot_ref(h, a, r), loc.at[h, a])

    for p in range(1, G):
        info_own(r, (r + p) % G, p).start()
    info_local = pltpu.make_async_copy(info_ref, ibuf.at[r], il)
    info_local.start()
    if pregathered:
        text_local = pltpu.make_async_copy(t_ref.at[:, :, group_cols(r)], text_group(grp), tls)
    else:
        text_local = pltpu.make_async_copy(
            t_ref.at[:, :, group_cols(r)], text_at((first + r) * trows, trows), tls)
        for p in range(1, G):
            text_own(r, (r + p) % G, p).start()
    text_local.start()
    for h in range(H):
        for a in range(3):
            for p in range(1, G):
                p1(h, a, r, (r + p) % G, p).start()
            p1_local(h, a).start()

    def hop_up(s):
        g = grp - (s - 1)
        return remote(text_group(g), text_group(g), ths.at[0, s - 1], thr.at[0, s - 1], up)

    def hop_dn(s):
        g = grp + (s - 1)
        return remote(text_group(g), text_group(g), ths.at[1, s - 1], thr.at[1, s - 1], dn)

    def got_up(s):
        g = grp - s
        return remote(text_group(g), text_group(g), ths.at[0, s - 1], thr.at[0, s - 1], dn)

    def got_dn(s):
        g = grp + s
        return remote(text_group(g), text_group(g), ths.at[1, s - 1], thr.at[1, s - 1], up)

    def send_text(s):
        @pl.when(has_up & (grp - (s - 1) >= 0))
        def _():
            hop_up(s).start()

        @pl.when(has_dn & (grp + (s - 1) < NG))
        def _():
            hop_dn(s).start()

    def recv_text(s):
        @pl.when(grp - s >= 0)
        def _():
            got_up(s).wait_recv()

        @pl.when(grp + s < NG)
        def _():
            got_dn(s).wait_recv()

    def drain_text(s):
        @pl.when(has_up & (grp - (s - 1) >= 0))
        def _():
            hop_up(s).wait_send()

        @pl.when(has_dn & (grp + (s - 1) < NG))
        def _():
            hop_dn(s).wait_send()

    lo = pl.ds(0, REACH * PB)
    own_top = pl.ds(G * PB, REACH * PB)
    own_bot = pl.ds(REACH * PB, REACH * PB)
    hi = pl.ds((REACH + G) * PB, REACH * PB)

    def kv_up(h):
        return remote(kv[h].at[:, own_top], kv[h].at[:, lo], zs.at[h, 0], zr.at[h, 0], up)

    def kv_dn(h):
        return remote(kv[h].at[:, own_bot], kv[h].at[:, hi], zs.at[h, 1], zr.at[h, 1], dn)

    def group_in(h):
        for a in range(3):
            for p in range(1, G):
                p1(h, a, (r + G - p) % G, r, p).wait_recv()
            p1_local(h, a).wait()

        @pl.when(has_up)
        def _():
            kv_up(h).start()

        @pl.when(has_dn)
        def _():
            kv_dn(h).start()

    if not pregathered:
        for p in range(1, G):
            text_own((r + G - p) % G, r, p).wait_recv()
    text_local.wait()
    hops = NG - 1
    if hops >= 1:
        send_text(1)
    for h in range(H):
        group_in(h)
        s = h + 1
        if s <= hops:
            recv_text(s)
            if s < hops:
                send_text(s + 1)
    for s in range(H + 1, hops + 1):
        recv_text(s)
        if s < hops:
            send_text(s + 1)

    for p in range(1, G):
        info_own((r + G - p) % G, r, p).wait_recv()
    info_local.wait()
    to_smem = pltpu.make_async_copy(ibuf, ismem, ism)
    to_smem.start()
    to_smem.wait()

    gain = math.log2(math.e) / math.sqrt(HD)
    base = (first - REACH) * PB

    def attend(h):
        def tile_body(j, carry):
            seg = ismem[j, PB, 0]
            cols = slice(h * HD, (h + 1) * HD)
            k_txt = txt[0, seg, :, cols]
            v_txt = txt[1, seg, :, cols]
            for b in range(PB):
                block = j * PB + b
                q = qb[h][block]
                places, bias = [], []
                for s in range(S):
                    entry = ismem[j, b, s]
                    used = entry >= 0
                    place = jnp.where(used, entry - base, REACH * PB + block)
                    places.append(jnp.clip(place, 0, (G + 2 * REACH) * PB - 1))
                    bias.append(jnp.where(used, 0.0, 1e30).astype(jnp.float32))
                keys = jnp.concatenate([kv[h][0, i] for i in places] + [k_txt], axis=0)
                scores = lax.dot_general(q, keys, (((1,), (1,)), ((), ())),
                                         preferred_element_type=jnp.float32)
                top = jnp.max(scores, axis=1, keepdims=True) * gain
                parts, total = [], None
                for s in range(S + TXT // BLK):
                    shift = top + bias[s] if s < S else top
                    w = jnp.exp2(scores[:, s * BLK : (s + 1) * BLK] * gain - shift)
                    total = w if total is None else total + w
                    parts.append(w.astype(jnp.bfloat16))
                values = jnp.concatenate([kv[h][1, i] for i in places] + [v_txt], axis=0)
                mixed = jnp.dot(jnp.concatenate(parts, axis=1), values,
                                preferred_element_type=jnp.float32)
                mixed = mixed / jnp.sum(total, axis=1, keepdims=True)
                ob[h][block] = mixed.astype(jnp.bfloat16)
            return carry

        lax.fori_loop(0, G, tile_body, 0)

    def out_copy(h, src_r, dst_t, p):
        return remote(ob[h].at[pl.ds(dst_t * PB, PB)], out_ref.at[:, :, head_cols(src_r, h)],
                      os_.at[h, p - 1], or_.at[h, p - 1], first + dst_t)

    def out_local(h):
        return pltpu.make_async_copy(ob[h].at[pl.ds(r * PB, PB)],
                                     out_ref.at[:, :, head_cols(r, h)], ol.at[h])

    for h in range(H):
        @pl.when(has_dn)
        def _():
            remote(kv[h].at[:, own_top], kv[h].at[:, lo], zs.at[h, 0], zr.at[h, 0], dn).wait_recv()

        @pl.when(has_up)
        def _():
            remote(kv[h].at[:, own_bot], kv[h].at[:, hi], zs.at[h, 1], zr.at[h, 1], up).wait_recv()

        attend(h)
        for p in range(1, G):
            out_copy(h, r, (r + p) % G, p).start()
        out_local(h).start()

    for p in range(1, G):
        info_own(r, (r + p) % G, p).wait_send()
        if not pregathered:
            text_own(r, (r + p) % G, p).wait_send()
    for s in range(1, hops + 1):
        drain_text(s)
    for h in range(H):
        for a in range(3):
            for p in range(1, G):
                p1(h, a, r, (r + p) % G, p).wait_send()

        @pl.when(has_up)
        def _():
            kv_up(h).wait_send()

        @pl.when(has_dn)
        def _():
            kv_dn(h).wait_send()

        for p in range(1, G):
            out_copy(h, r, (r + p) % G, p).wait_send()
            out_copy(h, (r + G - p) % G, r, p).wait_recv()
        out_local(h).wait()


def on_device(n, queries, latent_keys, latent_values, prompt_keyvals, block_lists, tile_segment):
    tok, width = queries.shape
    heads = width // HD
    PB = tok // BLK
    S = block_lists.shape[1]
    common = math.gcd(heads, n)
    G = min(d for d in range(REACH, common + 1) if common % d == 0)
    H = heads // G
    NG = n // G
    text = prompt_keyvals
    T = text.shape[1] * n
    pregathered = text.shape[1] % 16 != 0
    if pregathered:
        groups = [list(range(g * G, (g + 1) * G)) for g in range(NG)]
        text = lax.all_gather(text, "seq", axis=1, tiled=True, axis_index_groups=groups)
    info = jnp.zeros((8, 128), jnp.int32)
    info = info.at[:PB, :S].set(block_lists)
    info = info.at[PB, 0].set(tile_segment[0])
    blocks = lambda x: x.reshape(PB, BLK, width)
    bf = jnp.bfloat16
    dma = pltpu.SemaphoreType.DMA
    hops = max(NG - 1, 1)
    any_spec = pl.BlockSpec(memory_space=pl.ANY)
    out = pl.pallas_call(
        functools.partial(kernel, n, G, H, S, T, pregathered),
        out_shape=jax.ShapeDtypeStruct((PB, BLK, width), bf),
        in_specs=[pl.BlockSpec(memory_space=pltpu.VMEM)] + [any_spec] * 4,
        out_specs=any_spec,
        scratch_shapes=(
            [pltpu.VMEM((2, (G + 2 * REACH) * PB, BLK, HD), bf)] * H
            + [pltpu.VMEM((G * PB, BLK, HD), bf)] * H
            + [pltpu.VMEM((G * PB, BLK, HD), bf)] * H
            + [
                pltpu.VMEM((2, T // TXT, TXT, H * HD), bf),
                pltpu.VMEM((G, 8, 128), jnp.int32),
                pltpu.SMEM((G, 8, 128), jnp.int32),
                dma((H, 3, G - 1)), dma((H, 3, G - 1)), dma((H, 3)),
                dma((G - 1,)), dma((G - 1,)), dma,
                dma((G - 1,)), dma((G - 1,)), dma, dma,
                dma((H, 2)), dma((H, 2)),
                dma((2, hops)), dma((2, hops)),
                dma((H, G - 1)), dma((H, G - 1)), dma((H,)),
            ]
        ),
        compiler_params=pltpu.CompilerParams(collective_id=0, has_side_effects=True),
    )(info, blocks(queries), blocks(latent_keys), blocks(latent_values), text)
    return out.reshape(tok, width)


def solution(mesh):
    in_specs = (
        P(("cfg", "seq"), None),
        P(("cfg", "seq"), None),
        P(("cfg", "seq"), None),
        P(None, ("cfg", "seq"), None),
        P("seq", None),
        P("seq"),
    )
    out_specs = P(("cfg", "seq"), None)
    return jax.shard_map(
        functools.partial(on_device, mesh.shape["seq"]),
        mesh=mesh, in_specs=in_specs, out_specs=out_specs, check_vma=False,
    )
```

```python
import functools
import math

import jax
import jax.numpy as jnp
from jax import lax
from jax.experimental import pallas as pl
from jax.experimental.pallas import tpu as pltpu
from jax.sharding import PartitionSpec as P

HD = 128
BLK = 128
REACH = 3
TXT = 256
MESH = pl.DeviceIdType.MESH


def kernel(n, G, H, S, T, pregathered, info_ref, q_ref, k_ref, v_ref, t_ref, out_ref, *scratch):
    NG = n // G
    PB = q_ref.shape[0]
    kv = scratch[:H]
    qb = scratch[H : 2 * H]
    ob = scratch[2 * H : 3 * H]
    txt = scratch[3 * H : 4 * H]
    (ibuf, ismem, p1s, p1r, loc, t1s, t1r, tls, is_, ir, il, ism,
     zs, zr, hs1, hr1, ths, thr, os_, or_, ol) = scratch[4 * H :]
    me = lax.axis_index("seq")
    grp = me // G
    r = me % G
    first = grp * G
    has_up = grp + 1 < NG
    has_dn = grp > 0
    up, dn = me + G, me - G

    def remote(src, dst, ss, rs, dev):
        return pltpu.make_async_remote_copy(
            src_ref=src, dst_ref=dst, send_sem=ss, recv_sem=rs,
            device_id={"seq": dev}, device_id_type=MESH)

    def head_cols(t, h):
        return pl.ds(pl.multiple_of((t * H + h) * HD, HD), HD)

    barrier = pltpu.get_barrier_semaphore()
    for p in range(1, G):
        pl.semaphore_signal(barrier, inc=1, device_id={"seq": first + (r + p) % G}, device_id_type=MESH)

    @pl.when(has_up)
    def _():
        pl.semaphore_signal(barrier, inc=1, device_id={"seq": up}, device_id_type=MESH)

    @pl.when(has_dn)
    def _():
        pl.semaphore_signal(barrier, inc=1, device_id={"seq": dn}, device_id_type=MESH)

    count = (G - 1) + has_up.astype(jnp.int32) + has_dn.astype(jnp.int32)
    pl.semaphore_wait(barrier, count)

    mate = r + 1 - 2 * (r % 2)

    def to(p):
        if G == 4:
            return (mate, (r + 2) % G, (mate + 2) % G)[p - 1]
        return (r + p) % G

    def frm(p):
        if G == 4:
            return to(p)
        return (r + G - p) % G

    trows = t_ref.shape[1]
    pieces = 1 if pregathered else G
    prow = trows
    grows = prow * pieces

    def text_at(h, row, rows):
        return txt[h].at[:, row // TXT, pl.ds(pl.multiple_of(row % TXT, min(rows, TXT)), rows), :]

    def text_group(h, g):
        return text_at(h, g * grows, grows)

    def text_piece(h, g, i):
        return text_at(h, g * grows + i * prow, prow)

    own_piece = 0 if pregathered else r

    def text_swap(h, src_r, dst_t, p):
        return remote(t_ref.at[:, :, head_cols(dst_t, h)], text_piece(h, grp, src_r),
                      t1s.at[h, p - 1], t1r.at[h, p - 1], first + dst_t)

    def text_local(h):
        return pltpu.make_async_copy(
            t_ref.at[:, :, head_cols(r, h)], text_piece(h, grp, own_piece), tls.at[h])

    def info_own(src_r, dst_t, p):
        return remote(info_ref, ibuf.at[src_r], is_.at[p - 1], ir.at[p - 1], first + dst_t)

    def slot_ref(h, a, tile):
        if a == 2:
            return qb[h].at[pl.ds(tile * PB, PB)]
        return kv[h].at[a, pl.ds((REACH + tile) * PB, PB)]

    def p1(h, a, src_r, dst_t, p):
        src = (k_ref, v_ref, q_ref)[a].at[:, :, head_cols(dst_t, h)]
        return remote(src, slot_ref(h, a, src_r), p1s.at[h, a, p - 1], p1r.at[h, a, p - 1], first + dst_t)

    def p1_local(h, a):
        src = (k_ref, v_ref, q_ref)[a].at[:, :, head_cols(r, h)]
        return pltpu.make_async_copy(src, slot_ref(h, a, r), loc.at[h, a])

    def hop1(h, i, k, d):
        return remote(text_piece(h, grp, i), text_piece(h, grp, i), hs1.at[h, d, k], hr1.at[h, d, k],
                      up if d == 0 else dn)

    def send_piece(h, i, k):
        @pl.when(has_up)
        def _():
            hop1(h, i, k, 0).start()

        @pl.when(has_dn)
        def _():
            hop1(h, i, k, 1).start()

    def hop(h, s, g, d):
        return remote(text_group(h, g), text_group(h, g), ths.at[h, d, s - 2], thr.at[h, d, s - 2],
                      up if d == 0 else dn)

    def each_piece():
        return [(own_piece, 0)] + ([] if pregathered else [(frm(p), p) for p in range(1, G)])

    def send_text(h, s):
        @pl.when(has_up & (grp - (s - 1) >= 0))
        def _():
            hop(h, s, grp - (s - 1), 0).start()

        @pl.when(has_dn & (grp + (s - 1) < NG))
        def _():
            hop(h, s, grp + (s - 1), 1).start()

    def recv_text(h, s):
        @pl.when(grp - s >= 0)
        def _():
            if s == 1:
                for i, k in each_piece():
                    remote(text_piece(h, grp - 1, i), text_piece(h, grp - 1, i),
                           hs1.at[h, 0, k], hr1.at[h, 0, k], dn).wait_recv()
            else:
                hop(h, s, grp - s, 0).wait_recv()

        @pl.when(grp + s < NG)
        def _():
            if s == 1:
                for i, k in each_piece():
                    remote(text_piece(h, grp + 1, i), text_piece(h, grp + 1, i),
                           hs1.at[h, 1, k], hr1.at[h, 1, k], up).wait_recv()
            else:
                hop(h, s, grp + s, 1).wait_recv()

    def drain_text(h, s):
        @pl.when(has_up & (grp - (s - 1) >= 0))
        def _():
            if s == 1:
                for i, k in each_piece():
                    hop1(h, i, k, 0).wait_send()
            else:
                hop(h, s, grp - (s - 1), 0).wait_send()

        @pl.when(has_dn & (grp + (s - 1) < NG))
        def _():
            if s == 1:
                for i, k in each_piece():
                    hop1(h, i, k, 1).wait_send()
            else:
                hop(h, s, grp + (s - 1), 1).wait_send()

    for h in range(H):
        text_local(h).start()
    info_local = pltpu.make_async_copy(info_ref, ibuf.at[r], il)
    info_local.start()
    for h in range(H):
        for a in range(2):
            for p in range(1, G):
                p1(h, a, r, to(p), p).start()
            p1_local(h, a).start()
        if not pregathered:
            for p in range(1, G):
                text_swap(h, r, to(p), p).start()
        if h == 0:
            for p in range(1, G):
                info_own(r, to(p), p).start()
        for p in range(1, G):
            p1(h, 2, r, to(p), p).start()
        p1_local(h, 2).start()
    for h in range(H):
        text_local(h).wait()
        send_piece(h, own_piece, 0)

    lo = pl.ds(0, REACH * PB)
    own_top = pl.ds(G * PB, REACH * PB)
    own_bot = pl.ds(REACH * PB, REACH * PB)
    hi = pl.ds((REACH + G) * PB, REACH * PB)

    def kv_up(h, dev):
        return remote(kv[h].at[:, own_top], kv[h].at[:, lo], zs.at[h, 0], zr.at[h, 0], dev)

    def kv_dn(h, dev):
        return remote(kv[h].at[:, own_bot], kv[h].at[:, hi], zs.at[h, 1], zr.at[h, 1], dev)

    def group_in(h):
        for a in range(2):
            for p in range(1, G):
                p1(h, a, frm(p), r, p).wait_recv()
            p1_local(h, a).wait()

        @pl.when(has_up)
        def _():
            kv_up(h, up).start()

        @pl.when(has_dn)
        def _():
            kv_dn(h, dn).start()

        if not pregathered:
            for p in range(1, G):
                text_swap(h, frm(p), r, p).wait_recv()
                send_piece(h, frm(p), p)

    gain = math.log2(math.e) / math.sqrt(HD)
    base = (first - REACH) * PB

    def out_remote(h, src_r, dst_t):
        return remote(ob[h].at[pl.ds(dst_t * PB, PB)], out_ref.at[:, :, head_cols(src_r, h)],
                      os_.at[h, dst_t], or_.at[h, src_r], first + dst_t)

    def out_local(h):
        return pltpu.make_async_copy(ob[h].at[pl.ds(r * PB, PB)],
                                     out_ref.at[:, :, head_cols(r, h)], ol.at[h])

    def attend(h):
        def one_block(j, b):
            block = j * PB + b
            seg = ismem[j, PB, 0]
            q = qb[h][block]
            places, bias = [], []
            for s in range(S):
                entry = ismem[j, b, s]
                used = entry >= 0
                place = jnp.where(used, entry - base, REACH * PB + block)
                places.append(jnp.clip(place, 0, (G + 2 * REACH) * PB - 1))
                bias.append(jnp.where(used, 0.0, 1e30).astype(jnp.float32))
            keys = jnp.concatenate([kv[h][0, i] for i in places] + [txt[h][0, seg]], axis=0)
            scores = lax.dot_general(q, keys, (((1,), (1,)), ((), ())),
                                     preferred_element_type=jnp.float32)
            top = jnp.max(scores, axis=1, keepdims=True) * gain
            parts, total = [], None
            for s in range(S + TXT // BLK):
                shift = top + bias[s] if s < S else top
                w = jnp.exp2(scores[:, s * BLK : (s + 1) * BLK] * gain - shift)
                total = w if total is None else total + w
                parts.append(w.astype(jnp.bfloat16))
            values = jnp.concatenate([kv[h][1, i] for i in places] + [txt[h][1, seg]], axis=0)
            mixed = jnp.dot(jnp.concatenate(parts, axis=1), values,
                            preferred_element_type=jnp.float32)
            mixed = mixed / jnp.sum(total, axis=1, keepdims=True)
            ob[h][block] = mixed.astype(jnp.bfloat16)

        def tile_body(i, carry):
            j = (r + 1 + i) % G
            one_block(j, 0)

            @pl.when(i > 0)
            def _():
                out_remote(h, r, (r + i) % G).start()

            for b in range(1, PB):
                one_block(j, b)
            return carry

        lax.fori_loop(0, G, tile_body, 0)
        out_local(h).start()

    hops = NG - 1
    for t in range(H + hops):
        if t < H:
            group_in(t)
        for s in range(1, hops + 1):
            h = t - s
            if 0 <= h < H:
                recv_text(h, s)
                if s < hops:
                    send_text(h, s + 1)
        h = t - hops
        if h == 0:
            for p in range(1, G):
                info_own(frm(p), r, p).wait_recv()
            info_local.wait()
            to_smem = pltpu.make_async_copy(ibuf, ismem, ism)
            to_smem.start()
            to_smem.wait()
        if h >= 0:
            for p in range(1, G):
                p1(h, 2, frm(p), r, p).wait_recv()
            p1_local(h, 2).wait()

            @pl.when(has_dn)
            def _():
                kv_up(h, dn).wait_recv()

            @pl.when(has_up)
            def _():
                kv_dn(h, up).wait_recv()

            attend(h)

    for p in range(1, G):
        info_own(r, to(p), p).wait_send()
    for h in range(H):
        for s in range(1, hops + 1):
            drain_text(h, s)
        for a in range(3):
            for p in range(1, G):
                p1(h, a, r, to(p), p).wait_send()
        if not pregathered:
            for p in range(1, G):
                text_swap(h, r, to(p), p).wait_send()

        @pl.when(has_up)
        def _():
            kv_up(h, up).wait_send()

        @pl.when(has_dn)
        def _():
            kv_dn(h, dn).wait_send()

        for p in range(1, G):
            out_remote(h, r, to(p)).wait_send()
            out_remote(h, frm(p), r).wait_recv()
        out_local(h).wait()


def on_device(n, queries, latent_keys, latent_values, prompt_keyvals, block_lists, tile_segment):
    tok, width = queries.shape
    heads = width // HD
    PB = tok // BLK
    S = block_lists.shape[1]
    common = math.gcd(heads, n)
    G = min(d for d in range(REACH, common + 1) if common % d == 0)
    H = heads // G
    NG = n // G
    text = prompt_keyvals
    T = text.shape[1] * n
    pregathered = text.shape[1] % 16 != 0
    if pregathered:
        groups = [list(range(g * G, (g + 1) * G)) for g in range(NG)]
        text = lax.all_gather(text, "seq", axis=1, tiled=True, axis_index_groups=groups)
    info = jnp.zeros((8, 128), jnp.int32)
    info = info.at[:PB, :S].set(block_lists)
    info = info.at[PB, 0].set(tile_segment[0])
    blocks = lambda x: x.reshape(PB, BLK, width)
    bf = jnp.bfloat16
    dma = pltpu.SemaphoreType.DMA
    hops = max(NG - 1, 1)
    any_spec = pl.BlockSpec(memory_space=pl.ANY)
    out = pl.pallas_call(
        functools.partial(kernel, n, G, H, S, T, pregathered),
        out_shape=jax.ShapeDtypeStruct((PB, BLK, width), bf),
        in_specs=[pl.BlockSpec(memory_space=pltpu.VMEM)] + [any_spec] * 4,
        out_specs=any_spec,
        scratch_shapes=(
            [pltpu.VMEM((2, (G + 2 * REACH) * PB, BLK, HD), bf)] * H
            + [pltpu.VMEM((G * PB, BLK, HD), bf)] * H
            + [pltpu.VMEM((G * PB, BLK, HD), bf)] * H
            + [pltpu.VMEM((2, T // TXT, TXT, HD), bf)] * H
            + [
                pltpu.VMEM((G, 8, 128), jnp.int32),
                pltpu.SMEM((G, 8, 128), jnp.int32),
                dma((H, 3, G - 1)), dma((H, 3, G - 1)), dma((H, 3)),
                dma((H, G - 1)), dma((H, G - 1)), dma((H,)),
                dma((G - 1,)), dma((G - 1,)), dma, dma,
                dma((H, 2)), dma((H, 2)),
                dma((H, 2, G)), dma((H, 2, G)),
                dma((H, 2, hops)), dma((H, 2, hops)),
                dma((H, G)), dma((H, G)), dma((H,)),
            ]
        ),
        compiler_params=pltpu.CompilerParams(collective_id=0, has_side_effects=True),
    )(info, blocks(queries), blocks(latent_keys), blocks(latent_values), text)
    return out.reshape(tok, width)


def solution(mesh):
    in_specs = (
        P(("cfg", "seq"), None),
        P(("cfg", "seq"), None),
        P(("cfg", "seq"), None),
        P(None, ("cfg", "seq"), None),
        P("seq", None),
        P("seq"),
    )
    out_specs = P(("cfg", "seq"), None)
    return jax.shard_map(
        functools.partial(on_device, mesh.shape["seq"]),
        mesh=mesh, in_specs=in_specs, out_specs=out_specs, check_vma=False,
    )
```

```python
import functools
import math

import jax
import jax.numpy as jnp
from jax import lax
from jax.experimental import pallas as pl
from jax.experimental.pallas import tpu as pltpu
from jax.sharding import PartitionSpec as P

HD = 128
BLK = 128
REACH = 3
TXT = 256
MESH = pl.DeviceIdType.MESH


def kernel(n, G, H, S, T, pregathered, info_ref, q_ref, k_ref, v_ref, t_ref, out_ref, *scratch):
    NG = n // G
    PB = q_ref.shape[0]
    kv = scratch[:H]
    qb = scratch[H : 2 * H]
    ob = scratch[2 * H : 3 * H]
    txt = scratch[3 * H : 4 * H]
    (ibuf, ismem, p1s, p1r, loc, t1s, t1r, tls, is_, ir, il, ism,
     zs, zr, hs1, hr1, ths, thr, os_, or_, ol) = scratch[4 * H :]
    me = lax.axis_index("seq")
    grp = me // G
    r = me % G
    first = grp * G
    has_up = grp + 1 < NG
    has_dn = grp > 0
    up, dn = me + G, me - G

    def remote(src, dst, ss, rs, dev):
        return pltpu.make_async_remote_copy(
            src_ref=src, dst_ref=dst, send_sem=ss, recv_sem=rs,
            device_id={"seq": dev}, device_id_type=MESH)

    def head_cols(t, h):
        return pl.ds(pl.multiple_of((t * H + h) * HD, HD), HD)

    barrier = pltpu.get_barrier_semaphore()
    for p in range(1, G):
        pl.semaphore_signal(barrier, inc=1, device_id={"seq": first + (r + p) % G}, device_id_type=MESH)

    @pl.when(has_up)
    def _():
        pl.semaphore_signal(barrier, inc=1, device_id={"seq": up}, device_id_type=MESH)

    @pl.when(has_dn)
    def _():
        pl.semaphore_signal(barrier, inc=1, device_id={"seq": dn}, device_id_type=MESH)

    count = (G - 1) + has_up.astype(jnp.int32) + has_dn.astype(jnp.int32)
    pl.semaphore_wait(barrier, count)

    mate = r + 1 - 2 * (r % 2)

    def to(p):
        if G == 4:
            return (mate, (r + 2) % G, (mate + 2) % G)[p - 1]
        return (r + p) % G

    def frm(p):
        if G == 4:
            return to(p)
        return (r + G - p) % G

    trows = t_ref.shape[1]
    pieces = 1 if pregathered else G
    prow = trows
    grows = prow * pieces

    def text_at(h, row, rows):
        return txt[h].at[:, row // TXT, pl.ds(pl.multiple_of(row % TXT, min(rows, TXT)), rows), :]

    def text_group(h, g):
        return text_at(h, g * grows, grows)

    def text_piece(h, g, i):
        return text_at(h, g * grows + i * prow, prow)

    own_piece = 0 if pregathered else r

    def text_swap(h, src_r, dst_t, p):
        return remote(t_ref.at[:, :, head_cols(dst_t, h)], text_piece(h, grp, src_r),
                      t1s.at[h, p - 1], t1r.at[h, p - 1], first + dst_t)

    def text_local(h):
        return pltpu.make_async_copy(
            t_ref.at[:, :, head_cols(r, h)], text_piece(h, grp, own_piece), tls.at[h])

    def info_own(src_r, dst_t, p):
        return remote(info_ref, ibuf.at[src_r], is_.at[p - 1], ir.at[p - 1], first + dst_t)

    def slot_ref(h, a, tile):
        if a == 2:
            return qb[h].at[pl.ds(tile * PB, PB)]
        return kv[h].at[a, pl.ds((REACH + tile) * PB, PB)]

    def p1(h, a, src_r, dst_t, p):
        src = (k_ref, v_ref, q_ref)[a].at[:, :, head_cols(dst_t, h)]
        return remote(src, slot_ref(h, a, src_r), p1s.at[h, a, p - 1], p1r.at[h, a, p - 1], first + dst_t)

    def p1_local(h, a):
        src = (k_ref, v_ref, q_ref)[a].at[:, :, head_cols(r, h)]
        return pltpu.make_async_copy(src, slot_ref(h, a, r), loc.at[h, a])

    def hop1(h, i, k, d):
        return remote(text_piece(h, grp, i), text_piece(h, grp, i), hs1.at[h, d, k], hr1.at[h, d, k],
                      up if d == 0 else dn)

    def send_piece(h, i, k):
        @pl.when(has_up)
        def _():
            hop1(h, i, k, 0).start()

        @pl.when(has_dn)
        def _():
            hop1(h, i, k, 1).start()

    def hop(h, s, g, d):
        return remote(text_group(h, g), text_group(h, g), ths.at[h, d, s - 2], thr.at[h, d, s - 2],
                      up if d == 0 else dn)

    def each_piece():
        return [(own_piece, 0)] + ([] if pregathered else [(frm(p), p) for p in range(1, G)])

    def send_text(h, s):
        @pl.when(has_up & (grp - (s - 1) >= 0))
        def _():
            hop(h, s, grp - (s - 1), 0).start()

        @pl.when(has_dn & (grp + (s - 1) < NG))
        def _():
            hop(h, s, grp + (s - 1), 1).start()

    def recv_text(h, s):
        @pl.when(grp - s >= 0)
        def _():
            if s == 1:
                for i, k in each_piece():
                    remote(text_piece(h, grp - 1, i), text_piece(h, grp - 1, i),
                           hs1.at[h, 0, k], hr1.at[h, 0, k], dn).wait_recv()
            else:
                hop(h, s, grp - s, 0).wait_recv()

        @pl.when(grp + s < NG)
        def _():
            if s == 1:
                for i, k in each_piece():
                    remote(text_piece(h, grp + 1, i), text_piece(h, grp + 1, i),
                           hs1.at[h, 1, k], hr1.at[h, 1, k], up).wait_recv()
            else:
                hop(h, s, grp + s, 1).wait_recv()

    def drain_text(h, s):
        @pl.when(has_up & (grp - (s - 1) >= 0))
        def _():
            if s == 1:
                for i, k in each_piece():
                    hop1(h, i, k, 0).wait_send()
            else:
                hop(h, s, grp - (s - 1), 0).wait_send()

        @pl.when(has_dn & (grp + (s - 1) < NG))
        def _():
            if s == 1:
                for i, k in each_piece():
                    hop1(h, i, k, 1).wait_send()
            else:
                hop(h, s, grp + (s - 1), 1).wait_send()

    for h in range(H):
        text_local(h).start()
    info_local = pltpu.make_async_copy(info_ref, ibuf.at[r], il)
    info_local.start()
    if not pregathered:
        for h in range(H):
            text_swap(h, r, to(1), 1).start()
    for h in range(H):
        for a in range(2):
            for p in range(1, G):
                p1(h, a, r, to(p), p).start()
            p1_local(h, a).start()
        if h == 0:
            if not pregathered:
                for g in range(H):
                    for p in range(2, G):
                        text_swap(g, r, to(p), p).start()
            for p in range(1, G):
                info_own(r, to(p), p).start()
        for p in range(1, G):
            p1(h, 2, r, to(p), p).start()
        p1_local(h, 2).start()
    for h in range(H):
        text_local(h).wait()
        send_piece(h, own_piece, 0)

    def pass_pieces(h, ps):
        if not pregathered:
            for p in ps:
                text_swap(h, frm(p), r, p).wait_recv()
                send_piece(h, frm(p), p)

    for h in range(H):
        pass_pieces(h, [1])

    lo = pl.ds(0, REACH * PB)
    own_top = pl.ds(G * PB, REACH * PB)
    own_bot = pl.ds(REACH * PB, REACH * PB)
    hi = pl.ds((REACH + G) * PB, REACH * PB)

    def kv_up(h, dev):
        return remote(kv[h].at[:, own_top], kv[h].at[:, lo], zs.at[h, 0], zr.at[h, 0], dev)

    def kv_dn(h, dev):
        return remote(kv[h].at[:, own_bot], kv[h].at[:, hi], zs.at[h, 1], zr.at[h, 1], dev)

    def group_in(h):
        for a in range(2):
            for p in range(1, G):
                p1(h, a, frm(p), r, p).wait_recv()
            p1_local(h, a).wait()

        @pl.when(has_up)
        def _():
            kv_up(h, up).start()

        @pl.when(has_dn)
        def _():
            kv_dn(h, dn).start()

    gain = math.log2(math.e) / math.sqrt(HD)
    base = (first - REACH) * PB

    def out_remote(h, src_r, dst_t):
        return remote(ob[h].at[pl.ds(dst_t * PB, PB)], out_ref.at[:, :, head_cols(src_r, h)],
                      os_.at[h, dst_t], or_.at[h, src_r], first + dst_t)

    def out_local(h):
        return pltpu.make_async_copy(ob[h].at[pl.ds(r * PB, PB)],
                                     out_ref.at[:, :, head_cols(r, h)], ol.at[h])

    def attend(h):
        def one_block(j, b):
            block = j * PB + b
            seg = ismem[j, PB, 0]
            q = qb[h][block]
            places, bias = [], []
            for s in range(S):
                entry = ismem[j, b, s]
                used = entry >= 0
                place = jnp.where(used, entry - base, REACH * PB + block)
                places.append(jnp.clip(place, 0, (G + 2 * REACH) * PB - 1))
                bias.append(jnp.where(used, 0.0, 1e30).astype(jnp.float32))
            keys = jnp.concatenate([kv[h][0, i] for i in places] + [txt[h][0, seg]], axis=0)
            scores = lax.dot_general(q, keys, (((1,), (1,)), ((), ())),
                                     preferred_element_type=jnp.float32)
            top = jnp.max(scores, axis=1, keepdims=True) * gain
            parts, total = [], None
            for s in range(S + TXT // BLK):
                shift = top + bias[s] if s < S else top
                w = jnp.exp2(scores[:, s * BLK : (s + 1) * BLK] * gain - shift)
                total = w if total is None else total + w
                parts.append(w.astype(jnp.bfloat16))
            values = jnp.concatenate([kv[h][1, i] for i in places] + [txt[h][1, seg]], axis=0)
            mixed = jnp.dot(jnp.concatenate(parts, axis=1), values,
                            preferred_element_type=jnp.float32)
            mixed = mixed / jnp.sum(total, axis=1, keepdims=True)
            ob[h][block] = mixed.astype(jnp.bfloat16)

        def tile_body(i, carry):
            j = (r + 1 + i) % G
            one_block(j, 0)

            @pl.when(i > 0)
            def _():
                out_remote(h, r, (r + i) % G).start()

            for b in range(1, PB):
                one_block(j, b)
            return carry

        lax.fori_loop(0, G, tile_body, 0)
        out_local(h).start()

    hops = NG - 1
    group_in(0)
    for h in range(H):
        pass_pieces(h, range(2, G))
    for t in range(1, hops):
        if t < H:
            group_in(t)
        for h in range(H):
            recv_text(h, t)
            send_text(h, t + 1)
    for h in range(max(hops, 1), H):
        group_in(h)
    for p in range(1, G):
        info_own(frm(p), r, p).wait_recv()
    info_local.wait()
    to_smem = pltpu.make_async_copy(ibuf, ismem, ism)
    to_smem.start()
    to_smem.wait()
    for h in range(H):
        if hops >= 1:
            recv_text(h, hops)
        for p in range(1, G):
            p1(h, 2, frm(p), r, p).wait_recv()
        p1_local(h, 2).wait()

        @pl.when(has_dn)
        def _():
            kv_up(h, dn).wait_recv()

        @pl.when(has_up)
        def _():
            kv_dn(h, up).wait_recv()

        attend(h)

    for p in range(1, G):
        info_own(r, to(p), p).wait_send()
    for h in range(H):
        for s in range(1, hops + 1):
            drain_text(h, s)
        for a in range(3):
            for p in range(1, G):
                p1(h, a, r, to(p), p).wait_send()
        if not pregathered:
            for p in range(1, G):
                text_swap(h, r, to(p), p).wait_send()

        @pl.when(has_up)
        def _():
            kv_up(h, up).wait_send()

        @pl.when(has_dn)
        def _():
            kv_dn(h, dn).wait_send()

        for p in range(1, G):
            out_remote(h, r, to(p)).wait_send()
            out_remote(h, frm(p), r).wait_recv()
        out_local(h).wait()


def on_device(n, queries, latent_keys, latent_values, prompt_keyvals, block_lists, tile_segment):
    tok, width = queries.shape
    heads = width // HD
    PB = tok // BLK
    S = block_lists.shape[1]
    common = math.gcd(heads, n)
    G = min(d for d in range(REACH, common + 1) if common % d == 0)
    H = heads // G
    NG = n // G
    text = prompt_keyvals
    T = text.shape[1] * n
    pregathered = text.shape[1] % 16 != 0
    if pregathered:
        groups = [list(range(g * G, (g + 1) * G)) for g in range(NG)]
        text = lax.all_gather(text, "seq", axis=1, tiled=True, axis_index_groups=groups)
    info = jnp.zeros((8, 128), jnp.int32)
    info = info.at[:PB, :S].set(block_lists)
    info = info.at[PB, 0].set(tile_segment[0])
    blocks = lambda x: x.reshape(PB, BLK, width)
    bf = jnp.bfloat16
    dma = pltpu.SemaphoreType.DMA
    hops = max(NG - 1, 1)
    any_spec = pl.BlockSpec(memory_space=pl.ANY)
    out = pl.pallas_call(
        functools.partial(kernel, n, G, H, S, T, pregathered),
        out_shape=jax.ShapeDtypeStruct((PB, BLK, width), bf),
        in_specs=[any_spec] * 5,
        out_specs=any_spec,
        scratch_shapes=(
            [pltpu.VMEM((2, (G + 2 * REACH) * PB, BLK, HD), bf)] * H
            + [pltpu.VMEM((G * PB, BLK, HD), bf)] * H
            + [pltpu.VMEM((G * PB, BLK, HD), bf)] * H
            + [pltpu.VMEM((2, T // TXT, TXT, HD), bf)] * H
            + [
                pltpu.VMEM((G, 8, 128), jnp.int32),
                pltpu.SMEM((G, 8, 128), jnp.int32),
                dma((H, 3, G - 1)), dma((H, 3, G - 1)), dma((H, 3)),
                dma((H, G - 1)), dma((H, G - 1)), dma((H,)),
                dma((G - 1,)), dma((G - 1,)), dma, dma,
                dma((H, 2)), dma((H, 2)),
                dma((H, 2, G)), dma((H, 2, G)),
                dma((H, 2, hops)), dma((H, 2, hops)),
                dma((H, G)), dma((H, G)), dma((H,)),
            ]
        ),
        compiler_params=pltpu.CompilerParams(collective_id=0, has_side_effects=True),
    )(info, blocks(queries), blocks(latent_keys), blocks(latent_values), text)
    return out.reshape(tok, width)


def solution(mesh):
    in_specs = (
        P(("cfg", "seq"), None),
        P(("cfg", "seq"), None),
        P(("cfg", "seq"), None),
        P(None, ("cfg", "seq"), None),
        P("seq", None),
        P("seq"),
    )
    out_specs = P(("cfg", "seq"), None)
    return jax.shard_map(
        functools.partial(on_device, mesh.shape["seq"]),
        mesh=mesh, in_specs=in_specs, out_specs=out_specs, check_vma=False,
    )
```

```python
import functools
import math

import jax
import jax.numpy as jnp
from jax import lax
from jax.experimental import pallas as pl
from jax.experimental.pallas import tpu as pltpu
from jax.sharding import PartitionSpec as P

HD = 128
BLK = 128
REACH = 3
TXT = 256
MESH = pl.DeviceIdType.MESH


def kernel(n, G, H, S, T, pregathered, info_ref, q_ref, k_ref, v_ref, t_ref, out_ref, *scratch):
    NG = n // G
    PB = q_ref.shape[0]
    kv = scratch[:H]
    qb = scratch[H : 2 * H]
    ob = scratch[2 * H : 3 * H]
    txt = scratch[3 * H : 4 * H]
    (ibuf, ismem, p1s, p1r, loc, t1s, t1r, tls, is_, ir, il, ism,
     zs, zr, hs1, hr1, ths, thr, os_, or_, ol) = scratch[4 * H :]
    me = lax.axis_index("seq")
    grp = me // G
    r = me % G
    first = grp * G
    has_up = grp + 1 < NG
    has_dn = grp > 0
    up, dn = me + G, me - G

    def remote(src, dst, ss, rs, dev):
        return pltpu.make_async_remote_copy(
            src_ref=src, dst_ref=dst, send_sem=ss, recv_sem=rs,
            device_id={"seq": dev}, device_id_type=MESH)

    def head_cols(t, h):
        return pl.ds(pl.multiple_of((t * H + h) * HD, HD), HD)

    barrier = pltpu.get_barrier_semaphore()
    for p in range(1, G):
        pl.semaphore_signal(barrier, inc=1, device_id={"seq": first + (r + p) % G}, device_id_type=MESH)

    @pl.when(has_up)
    def _():
        pl.semaphore_signal(barrier, inc=1, device_id={"seq": up}, device_id_type=MESH)

    @pl.when(has_dn)
    def _():
        pl.semaphore_signal(barrier, inc=1, device_id={"seq": dn}, device_id_type=MESH)

    count = (G - 1) + has_up.astype(jnp.int32) + has_dn.astype(jnp.int32)
    pl.semaphore_wait(barrier, count)

    mate = r + 1 - 2 * (r % 2)

    def to(p):
        if G == 4:
            return (mate, (r + 2) % G, (mate + 2) % G)[p - 1]
        return (r + p) % G

    def frm(p):
        if G == 4:
            return to(p)
        return (r + G - p) % G

    trows = t_ref.shape[1]
    pieces = 1 if pregathered else G
    prow = trows
    grows = prow * pieces

    def text_at(h, row, rows):
        return txt[h].at[:, row // TXT, pl.ds(pl.multiple_of(row % TXT, min(rows, TXT)), rows), :]

    def text_group(h, g):
        return text_at(h, g * grows, grows)

    def text_piece(h, g, i):
        return text_at(h, g * grows + i * prow, prow)

    own_piece = 0 if pregathered else r

    def text_swap(h, src_r, dst_t, p):
        return remote(t_ref.at[:, :, head_cols(dst_t, h)], text_piece(h, grp, src_r),
                      t1s.at[h, p - 1], t1r.at[h, p - 1], first + dst_t)

    def text_local(h):
        return pltpu.make_async_copy(
            t_ref.at[:, :, head_cols(r, h)], text_piece(h, grp, own_piece), tls.at[h])

    def info_own(src_r, dst_t, p):
        return remote(info_ref, ibuf.at[src_r], is_.at[p - 1], ir.at[p - 1], first + dst_t)

    def slot_ref(h, a, tile):
        if a == 2:
            return qb[h].at[pl.ds(tile * PB, PB)]
        return kv[h].at[a, pl.ds((REACH + tile) * PB, PB)]

    def p1(h, a, src_r, dst_t, p):
        src = (k_ref, v_ref, q_ref)[a].at[:, :, head_cols(dst_t, h)]
        return remote(src, slot_ref(h, a, src_r), p1s.at[h, a, p - 1], p1r.at[h, a, p - 1], first + dst_t)

    def p1_local(h, a):
        src = (k_ref, v_ref, q_ref)[a].at[:, :, head_cols(r, h)]
        return pltpu.make_async_copy(src, slot_ref(h, a, r), loc.at[h, a])

    def hop1(h, i, k, d):
        src = t_ref.at[:, :, head_cols(r, h)] if k == 0 else text_piece(h, grp, i)
        return remote(src, text_piece(h, grp, i), hs1.at[h, d, k], hr1.at[h, d, k],
                      up if d == 0 else dn)

    def send_piece(h, i, k):
        @pl.when(has_up)
        def _():
            hop1(h, i, k, 0).start()

        @pl.when(has_dn)
        def _():
            hop1(h, i, k, 1).start()

    def hop(h, s, g, d):
        return remote(text_group(h, g), text_group(h, g), ths.at[h, d, s - 2], thr.at[h, d, s - 2],
                      up if d == 0 else dn)

    def each_piece():
        return [(own_piece, 0)] + ([] if pregathered else [(frm(p), p) for p in range(1, G)])

    def send_text(h, s):
        @pl.when(has_up & (grp - (s - 1) >= 0))
        def _():
            hop(h, s, grp - (s - 1), 0).start()

        @pl.when(has_dn & (grp + (s - 1) < NG))
        def _():
            hop(h, s, grp + (s - 1), 1).start()

    def recv_text(h, s):
        @pl.when(grp - s >= 0)
        def _():
            if s == 1:
                for i, k in each_piece():
                    remote(text_piece(h, grp - 1, i), text_piece(h, grp - 1, i),
                           hs1.at[h, 0, k], hr1.at[h, 0, k], dn).wait_recv()
            else:
                hop(h, s, grp - s, 0).wait_recv()

        @pl.when(grp + s < NG)
        def _():
            if s == 1:
                for i, k in each_piece():
                    remote(text_piece(h, grp + 1, i), text_piece(h, grp + 1, i),
                           hs1.at[h, 1, k], hr1.at[h, 1, k], up).wait_recv()
            else:
                hop(h, s, grp + s, 1).wait_recv()

    def drain_text(h, s):
        @pl.when(has_up & (grp - (s - 1) >= 0))
        def _():
            if s == 1:
                for i, k in each_piece():
                    hop1(h, i, k, 0).wait_send()
            else:
                hop(h, s, grp - (s - 1), 0).wait_send()

        @pl.when(has_dn & (grp + (s - 1) < NG))
        def _():
            if s == 1:
                for i, k in each_piece():
                    hop1(h, i, k, 1).wait_send()
            else:
                hop(h, s, grp + (s - 1), 1).wait_send()

    for h in range(H):
        send_piece(h, own_piece, 0)
    for h in range(H):
        text_local(h).start()
    info_local = pltpu.make_async_copy(info_ref, ibuf.at[r], il)
    info_local.start()
    if not pregathered:
        for h in range(H):
            text_swap(h, r, to(1), 1).start()
    for h in range(H):
        for a in range(2):
            for p in range(1, G):
                p1(h, a, r, to(p), p).start()
            p1_local(h, a).start()
        if h == 0:
            if not pregathered:
                for g in range(H):
                    for p in range(2, G):
                        text_swap(g, r, to(p), p).start()
            for p in range(1, G):
                info_own(r, to(p), p).start()
        for p in range(1, G):
            p1(h, 2, r, to(p), p).start()
        p1_local(h, 2).start()
    for h in range(H):
        text_local(h).wait()

    def pass_pieces(h, ps):
        if not pregathered:
            for p in ps:
                text_swap(h, frm(p), r, p).wait_recv()
                send_piece(h, frm(p), p)

    for h in range(H):
        pass_pieces(h, [1])

    lo = pl.ds(0, REACH * PB)
    own_top = pl.ds(G * PB, REACH * PB)
    own_bot = pl.ds(REACH * PB, REACH * PB)
    hi = pl.ds((REACH + G) * PB, REACH * PB)

    def kv_up(h, dev):
        return remote(kv[h].at[:, own_top], kv[h].at[:, lo], zs.at[h, 0], zr.at[h, 0], dev)

    def kv_dn(h, dev):
        return remote(kv[h].at[:, own_bot], kv[h].at[:, hi], zs.at[h, 1], zr.at[h, 1], dev)

    def group_in(h):
        for a in range(2):
            for p in range(1, G):
                p1(h, a, frm(p), r, p).wait_recv()
            p1_local(h, a).wait()

        @pl.when(has_up)
        def _():
            kv_up(h, up).start()

        @pl.when(has_dn)
        def _():
            kv_dn(h, dn).start()

    gain = math.log2(math.e) / math.sqrt(HD)
    base = (first - REACH) * PB

    def out_remote(h, src_r, dst_t):
        return remote(ob[h].at[pl.ds(dst_t * PB, PB)], out_ref.at[:, :, head_cols(src_r, h)],
                      os_.at[h, dst_t], or_.at[h, src_r], first + dst_t)

    def out_local(h):
        return pltpu.make_async_copy(ob[h].at[pl.ds(r * PB, PB)],
                                     out_ref.at[:, :, head_cols(r, h)], ol.at[h])

    def attend(h):
        def one_block(j, b):
            block = j * PB + b
            seg = ismem[j, PB, 0]
            q = qb[h][block]
            places, bias = [], []
            for s in range(S):
                entry = ismem[j, b, s]
                used = entry >= 0
                place = jnp.where(used, entry - base, REACH * PB + block)
                places.append(jnp.clip(place, 0, (G + 2 * REACH) * PB - 1))
                bias.append(jnp.where(used, 0.0, 1e30).astype(jnp.float32))
            keys = jnp.concatenate([kv[h][0, i] for i in places] + [txt[h][0, seg]], axis=0)
            scores = lax.dot_general(q, keys, (((1,), (1,)), ((), ())),
                                     preferred_element_type=jnp.float32)
            top = jnp.max(scores, axis=1, keepdims=True) * gain
            parts, total = [], None
            for s in range(S + TXT // BLK):
                shift = top + bias[s] if s < S else top
                w = jnp.exp2(scores[:, s * BLK : (s + 1) * BLK] * gain - shift)
                total = w if total is None else total + w
                parts.append(w.astype(jnp.bfloat16))
            values = jnp.concatenate([kv[h][1, i] for i in places] + [txt[h][1, seg]], axis=0)
            mixed = jnp.dot(jnp.concatenate(parts, axis=1), values,
                            preferred_element_type=jnp.float32)
            mixed = mixed / jnp.sum(total, axis=1, keepdims=True)
            ob[h][block] = mixed.astype(jnp.bfloat16)

        def tile_body(i, carry):
            j = (r + 1 + i) % G
            one_block(j, 0)

            @pl.when(i > 0)
            def _():
                out_remote(h, r, (r + i) % G).start()

            for b in range(1, PB):
                one_block(j, b)
            return carry

        lax.fori_loop(0, G, tile_body, 0)
        out_local(h).start()

    hops = NG - 1
    group_in(0)
    for h in range(H):
        pass_pieces(h, range(2, G))
    for t in range(1, hops):
        if t < H:
            group_in(t)
        for h in range(H):
            recv_text(h, t)
            send_text(h, t + 1)
    for h in range(max(hops, 1), H):
        group_in(h)
    for p in range(1, G):
        info_own(frm(p), r, p).wait_recv()
    info_local.wait()
    to_smem = pltpu.make_async_copy(ibuf, ismem, ism)
    to_smem.start()
    to_smem.wait()
    for h in range(H):
        if hops >= 1:
            recv_text(h, hops)
        for p in range(1, G):
            p1(h, 2, frm(p), r, p).wait_recv()
        p1_local(h, 2).wait()

        @pl.when(has_dn)
        def _():
            kv_up(h, dn).wait_recv()

        @pl.when(has_up)
        def _():
            kv_dn(h, up).wait_recv()

        attend(h)

    for p in range(1, G):
        info_own(r, to(p), p).wait_send()
    for h in range(H):
        for s in range(1, hops + 1):
            drain_text(h, s)
        for a in range(3):
            for p in range(1, G):
                p1(h, a, r, to(p), p).wait_send()
        if not pregathered:
            for p in range(1, G):
                text_swap(h, r, to(p), p).wait_send()

        @pl.when(has_up)
        def _():
            kv_up(h, up).wait_send()

        @pl.when(has_dn)
        def _():
            kv_dn(h, dn).wait_send()

        for p in range(1, G):
            out_remote(h, r, to(p)).wait_send()
            out_remote(h, frm(p), r).wait_recv()
        out_local(h).wait()


def on_device(n, queries, latent_keys, latent_values, prompt_keyvals, block_lists, tile_segment):
    tok, width = queries.shape
    heads = width // HD
    PB = tok // BLK
    S = block_lists.shape[1]
    common = math.gcd(heads, n)
    G = min(d for d in range(REACH, common + 1) if common % d == 0)
    H = heads // G
    NG = n // G
    text = prompt_keyvals
    T = text.shape[1] * n
    pregathered = text.shape[1] % 16 != 0
    if pregathered:
        groups = [list(range(g * G, (g + 1) * G)) for g in range(NG)]
        text = lax.all_gather(text, "seq", axis=1, tiled=True, axis_index_groups=groups)
    info = jnp.pad(block_lists, ((0, 8 - PB), (0, 128 - S)))
    info = info + jnp.pad(tile_segment[None, :1], ((PB, 7 - PB), (0, 127)))
    blocks = lambda x: x.reshape(PB, BLK, width)
    bf = jnp.bfloat16
    dma = pltpu.SemaphoreType.DMA
    hops = max(NG - 1, 1)
    any_spec = pl.BlockSpec(memory_space=pl.ANY)
    out = pl.pallas_call(
        functools.partial(kernel, n, G, H, S, T, pregathered),
        out_shape=jax.ShapeDtypeStruct((PB, BLK, width), bf),
        in_specs=[any_spec] * 5,
        out_specs=any_spec,
        scratch_shapes=(
            [pltpu.VMEM((2, (G + 2 * REACH) * PB, BLK, HD), bf)] * H
            + [pltpu.VMEM((G * PB, BLK, HD), bf)] * H
            + [pltpu.VMEM((G * PB, BLK, HD), bf)] * H
            + [pltpu.VMEM((2, T // TXT, TXT, HD), bf)] * H
            + [
                pltpu.VMEM((G, 8, 128), jnp.int32),
                pltpu.SMEM((G, 8, 128), jnp.int32),
                dma((H, 3, G - 1)), dma((H, 3, G - 1)), dma((H, 3)),
                dma((H, G - 1)), dma((H, G - 1)), dma((H,)),
                dma((G - 1,)), dma((G - 1,)), dma, dma,
                dma((H, 2)), dma((H, 2)),
                dma((H, 2, G)), dma((H, 2, G)),
                dma((H, 2, hops)), dma((H, 2, hops)),
                dma((H, G)), dma((H, G)), dma((H,)),
            ]
        ),
        compiler_params=pltpu.CompilerParams(collective_id=0, has_side_effects=True),
    )(info, blocks(queries), blocks(latent_keys), blocks(latent_values), text)
    return out.reshape(tok, width)


def solution(mesh):
    in_specs = (
        P(("cfg", "seq"), None),
        P(("cfg", "seq"), None),
        P(("cfg", "seq"), None),
        P(None, ("cfg", "seq"), None),
        P("seq", None),
        P("seq"),
    )
    out_specs = P(("cfg", "seq"), None)
    return jax.shard_map(
        functools.partial(on_device, mesh.shape["seq"]),
        mesh=mesh, in_specs=in_specs, out_specs=out_specs, check_vma=False,
    )
```
